32 devices in a mesh: dp: 16 (over z, y, core), mp: 2 (over x).
Axes of the slice: x: 2, y: 2, z: 4, core: 2. Of those that a mesh axis runs over, the one named last changes fastest.
Arguments:
- tokens: bfloat16 [2048, 2048], P('dp', 'mp'), may hold values from -32 to 32
- lengths: int32 [4], replicated, may hold values from 1 to 1536, 2048 in all
- keep_mask: int32 [2048], replicated, may hold values 0 or 1
- routes: int32 [2048, 8], P('dp'), may hold values from 0 to 63, all different within a row; in each aligned block of 128 rows (0 to 127, 128 to 255, ...) at most 32 rows name the same one
- attention_gain: float32 [2048], replicated, may hold values from 0.1 to 1.9
- mixture_gain: float32 [2048], P('mp'), may hold values from 0.1 to 1.9
- query_gain: float32 [128], replicated, may hold values from 0.5 to 8, as said below
- key_gain: float32 [128], replicated, may hold values from 0.5 to 8, as said below
- query_weight: bfloat16 [2048, 2048], P('dp', 'mp'), may hold values from -0.125 to 0.125
- key_weight: bfloat16 [2048, 2048], P('dp', 'mp'), may hold values from -0.125 to 0.125
- value_weight: bfloat16 [2048, 2048], P('dp', 'mp'), may hold values from -0.125 to 0.125
- output_weight: bfloat16 [2048, 2048], P('mp', 'dp'), may hold values from -0.1875 to 0.1875
- router_weight: float32 [2048, 64], P('mp'), may hold values from -0.125 to 0.125
- expert_gate: bfloat16 [16, 2048, 4096], P('dp', None, 'mp'), may hold values from -0.125 to 0.125
- expert_up: bfloat16 [16, 2048, 4096], P('dp', None, 'mp'), may hold values from -0.125 to 0.125
- expert_down: bfloat16 [16, 4096, 2048], P('dp', 'mp'), may hold values from -0.25 to 0.25
Outputs:
- layer_output: bfloat16 [2048, 2048], P('dp', 'mp')
The draws below stay inside these ranges and needn't reach their ends.
Inputs may be any that keep to these rules, and one draw needn't show every extreme that they name: The lengths sum to 2048; exactly one is 1536. `routes`: each row names 8 different experts. Within each aligned block of 128 rows (the rows of one index of dp) no expert is named by more than 32 rows, a bound that some block reaches. `query_gain`: Positive. `key_gain`: Positive.
All inputs are finite; a program needn't handle non-finite values.
Results may differ from the reference program's by a relative error of at most 0.012.
The reference program's roundings to bfloat16 on the way (of `normed_in`, `values`, `attended`, `residual`, `mixed_in`, `hidden` and `expert_out`) count: a program that leaves them out, or rounds other values in their place, can miss the bound.
Values may be sent and summed in bfloat16 or wider, within the bound.
A program may use at most 128 MiB of HBM per device.

```python
import math
import jax
import jax.numpy as jnp
import numpy as np
from jax import lax

D = 2048
HEADS = 16
HEAD_DIM = 128
FF = 1024
EXPERTS = 64
TOPK = 8
REQUESTS = 4
TOK_DEV = 128
TOKENS = 2048
LONG = 1536
CAP = 32
EXP_DEV = 4
SPLIT = 1
N_DP = 16


def draw_tokens(key, part):
    key_base = jax.random.fold_in(key, 101)
    key_cols = jax.random.fold_in(key, 102)
    key_rows = jax.random.fold_in(key, 103)
    ramp = jnp.arange(D, dtype=jnp.float32) / D
    col_scale = 0.6 * jnp.exp(jnp.log(3.0) * ramp) * jnp.exp(jax.random.uniform(key_cols, (D,), jnp.float32, -0.35, 0.35))
    row_scale = jnp.exp(jax.random.uniform(key_rows, (TOKENS, 1), jnp.float32, jnp.log(0.5), jnp.log(2.0)))
    base_vals = jnp.clip(jax.random.normal(key_base, (TOKENS, D), jnp.float32), -5.0, 5.0)
    return (base_vals * row_scale * col_scale[None, :]).astype(jnp.bfloat16)


def draw_query_gain(key, part):
    sub_key = jax.random.fold_in(key, 201)
    gains = jnp.exp(jax.random.uniform(sub_key, (HEAD_DIM,), jnp.float32, jnp.log(1.6), jnp.log(3.2)))
    return gains


def draw_key_gain(key, part):
    sub_key = jax.random.fold_in(key, 202)
    gains = jnp.exp(jax.random.uniform(sub_key, (HEAD_DIM,), jnp.float32, jnp.log(1.6), jnp.log(3.2)))
    return gains


def touch_ends(values, rng, low, largest):
    extent = values.shape
    spot = [jax.random.randint(jax.random.fold_in(rng, axis), (), 0, extent[axis]) for axis in range(len(extent))]
    values = values.at[tuple(spot)].set(low)
    longest = extent.index(max(extent))
    spot[longest] = (spot[longest] + 1) % extent[longest]
    return values.at[tuple(spot)].set(largest)


def spiked(drawn, own_key, source, target, blocks, factor):
    def block_of(dim):
        return (jnp.arange(drawn.shape[dim]) // (drawn.shape[dim] // blocks)).reshape((-1,) + (1,) * (drawn.ndim - 1 - dim))

    one_side = jax.random.permutation(own_key, blocks)[block_of(target)]
    second = (block_of(target) + blocks // 2) % blocks
    return jnp.where((block_of(source) == one_side) | (block_of(source) == second), factor * drawn, drawn)


def block_levels(own_key, extent, split, low, top_value):
    def one(dim, parts):
        draws = jax.random.uniform(jax.random.fold_in(jax.random.fold_in(own_key, 6), dim), (parts,), jnp.float32, low / len(split), top_value / len(split))
        return jnp.repeat(jnp.exp(draws), extent[dim] // parts).reshape((-1,) + (1,) * (len(extent) - dim - 1))

    level = one(*split[0])
    for cut in split[1:]:
        level = level * one(*cut)
    return level


def split_up(number_of, total, reach, skew):
    weights = [(1 << 20) // math.isqrt(rank ** skew) + 1 for rank in range(2, number_of + 1)]
    rest, holding = total - reach - (number_of - 1), [1] * (number_of - 1)
    while rest > 0:
        candidates = [i for i in range(number_of - 1) if holding[i] < reach]
        whole, remaining = sum([weights[i] for i in candidates]), rest
        for i in candidates:
            addition = min(reach - holding[i], max(1, remaining * weights[i] // whole), rest)
            holding[i] = holding[i] + addition
            rest = rest - addition
    return np.array([reach] + holding)


def ragged_sizes(stream_key, count, total, bound, slope):
    if count == 2:
        one = jax.random.randint(stream_key, (), max(1, total - bound), min(bound, total - 1) + 1)
        return jnp.stack([one, total - one])
    sizes = jnp.asarray(split_up(count, total, bound, slope), jnp.int32)
    twos = (count - 1) // 2
    donor, receiver = sizes[1:1 + 2 * twos:2], sizes[2:2 + 2 * twos:2]
    slack = jnp.minimum(donor - 1, bound - receiver)
    moved = jax.random.randint(jax.random.fold_in(stream_key, 1), (twos,), 0, 1 << 20) % (slack + 1)
    sizes = sizes.at[1:1 + 2 * twos:2].set(donor - moved).at[2:2 + 2 * twos:2].set(receiver + moved)
    return sizes[jax.random.permutation(jax.random.fold_in(stream_key, 2), count)]


def assign_block(key, own, number, rows, number_of, top, bound, slope):
    ranking = jax.random.permutation(key, number_of)
    crowded, usual = portions_of(number_of, rows * top, bound, slope, True), portions_of(number_of, rows * top, bound, slope, False)
    places = jnp.arange(number_of)

    def named(sizes, turn):
        used = int((sizes > 0).sum())
        fixed = max(1, used // 4)
        shifted = fixed + (places - fixed + turn * (used - fixed)) % max(1, number_of - fixed)
        return jnp.zeros((number_of,), jnp.int32).at[ranking[jnp.where(places < fixed, places, shifted)]].set(jnp.asarray(sizes, jnp.int32))

    sizes = jnp.where(number % 4 == 0, named(crowded, number // 4), named(usual, number - number // 4 - 1))
    mixed = jax.random.permutation(jax.random.fold_in(own, 3), number_of)
    donor, sink = mixed[0:number_of // 2 * 2:2], mixed[1:number_of // 2 * 2:2]
    slack = jnp.minimum(sizes[donor] - 1, bound - sizes[sink]) // 2
    slack = jnp.where((donor == ranking[0]) | (sink == ranking[0]) | (sizes[sink] == 0), 0, jnp.maximum(slack, 0))
    shifted = jax.random.randint(jax.random.fold_in(own, 4), (number_of // 2,), 0, 1 << 20) % (slack + 1)
    sizes = sizes.at[donor].add(-shifted).at[sink].add(shifted)
    labels = jnp.searchsorted(jnp.cumsum(sizes), jnp.arange(rows * top), side="right").astype(jnp.int32)
    table = labels.reshape(top, rows).T
    table = table[jax.random.permutation(jax.random.fold_in(own, 1), rows)]
    turn = jax.random.randint(jax.random.fold_in(own, 2), (rows, 1), 0, top)
    return jnp.take_along_axis(table, (jnp.arange(top)[None, :] + turn) % top, axis=1)


def portions_of(amount, total, bound, skew, full):
    loads = [(1 << 20) // math.isqrt(rank ** skew) + 1 for rank in range(1, amount + 1)]
    largest = bound if full else min(bound, max(-(-total // amount), total * loads[0] // sum(loads)))
    least = 1 if total - largest >= amount - 1 else 0
    holding, surplus = [largest] + [least] * (amount - 1), total - largest - least * (amount - 1)
    while surplus > 0:
        free = [i for i in range(1, amount) if holding[i] < largest] or [i for i in range(1, amount) if holding[i] < bound]
        pool, budget = sum([loads[i] for i in free]), surplus
        for i in free:
            extra = min(bound - holding[i], max(1, budget * loads[i] // pool), surplus)
            holding[i] = holding[i] + extra
            surplus = surplus - extra
    return np.array(holding)


def bell_draw(key, dims, deviation, bound, pieces=(), kind=jnp.bfloat16):
    loudness = block_levels(key, dims, pieces, -0.22, 0.18) if pieces else 1.0
    array = jax.random.normal(key, dims, jnp.float32) * deviation * loudness
    return jnp.minimum(jnp.maximum(array, -bound), bound).astype(kind)


def heavy_noise(rng, extent, scale, most, cuts, heavy, kind=jnp.bfloat16):
    drawn = scale * jax.random.normal(rng, extent, jnp.float32)
    if cuts:
        drawn = drawn * block_levels(rng, extent, cuts, -0.22, 0.18)
    return jnp.clip(spiked(drawn, jax.random.fold_in(rng, 3), *heavy), -most, most).astype(kind)


def setup_inputs(seed: int = 0) -> dict:
    key_of = jax.random.split(jax.random.key(seed), 17)
    tokens = draw_tokens(jax.random.fold_in(key_of[16], 71), 0)
    lengths = ragged_sizes(key_of[1], REQUESTS, TOKENS, LONG, 2).astype(jnp.int32)
    keep_mask = touch_ends((jax.random.randint(key_of[2], (TOKENS,), 0, 8) < 7).astype(jnp.int32), jax.random.fold_in(key_of[2], 1), 0, 1)
    routes_keys = jax.random.split(jax.random.fold_in(key_of[3], 1), TOKENS // TOK_DEV)
    routes_turns = jax.random.permutation(jax.random.fold_in(key_of[3], 3), TOKENS // TOK_DEV)
    routes = jax.vmap(lambda own, number: assign_block(jax.random.fold_in(key_of[3], 2), own, number, TOK_DEV, EXPERTS, TOPK, CAP, 2))(routes_keys, routes_turns).reshape((TOKENS, TOPK))
    attention_gain = jnp.clip(1.0 + 0.18 * jax.random.normal(key_of[4], (D,), jnp.float32), 0.1, 1.9)
    mixture_gain = jnp.clip(1.0 + 0.18 * jax.random.normal(key_of[5], (D,), jnp.float32), 0.1, 1.9)
    query_gain = draw_query_gain(jax.random.fold_in(key_of[16], 71), 0)
    key_gain = draw_key_gain(jax.random.fold_in(key_of[16], 71), 0)
    query_weight = bell_draw(key_of[8], (D, D), D ** -0.5, 0.125, ((0, 16), (1, 2)))
    key_weight = bell_draw(key_of[9], (D, D), D ** -0.5, 0.125, ((0, 16), (1, 2)))
    value_weight = bell_draw(key_of[10], (D, D), D ** -0.5, 0.125, ((0, 16), (1, 2)))
    output_weight = heavy_noise(key_of[11], (D, D), D ** -0.5, 0.1875, ((0, 2), (1, 16)), (0, 1, 16, 2.0))
    router_weight = bell_draw(key_of[12], (D, EXPERTS), D ** -0.5, 0.125, ((0, 2),), jnp.float32)
    expert_gate = bell_draw(key_of[13], (N_DP, D, EXP_DEV * FF), D ** -0.5, 0.125, ((0, 16), (2, 2)))
    expert_up = bell_draw(key_of[14], (N_DP, D, EXP_DEV * FF), D ** -0.5, 0.125, ((0, 16), (2, 2)))
    expert_down = heavy_noise(key_of[15], (N_DP, EXP_DEV * FF, D), FF ** -0.5, 0.25, ((0, 16), (1, 2)), (1, 2, 2, 2.0))
    return dict(tokens=tokens, lengths=lengths, keep_mask=keep_mask, routes=routes, attention_gain=attention_gain, mixture_gain=mixture_gain, query_gain=query_gain, key_gain=key_gain, query_weight=query_weight, key_weight=key_weight, value_weight=value_weight, output_weight=output_weight, router_weight=router_weight, expert_gate=expert_gate, expert_up=expert_up, expert_down=expert_down)


EPS = 1e-06
ROPE_BASE = 10000.0
NEG = -1e+30

def rope_tables(position):
    halves = HEAD_DIM // 2
    exponent = jnp.arange(halves, dtype=jnp.float32) * (2.0 / HEAD_DIM)
    frequency = jnp.power(jnp.float32(ROPE_BASE), -exponent)
    angle = position.astype(jnp.float32)[:, None] * frequency[None, :]
    cos_table = jnp.cos(angle)
    sin_table = jnp.sin(angle)
    return (jnp.concatenate([cos_table, cos_table], 1), jnp.concatenate([sin_table, sin_table], 1))

def head_prep(projected, head_gain, cos_table, sin_table):
    row_count = projected.shape[0]
    per_head = projected.reshape(row_count, -1, HEAD_DIM)
    normed = per_head * lax.rsqrt(lax.optimization_barrier(jnp.mean(per_head * per_head, axis=2, keepdims=True)) + EPS) * head_gain
    halves = HEAD_DIM // 2
    rotated = jnp.concatenate([-normed[:, :, halves:], normed[:, :, :halves]], 2)
    turned = normed * cos_table[:, None, :] + rotated * sin_table[:, None, :]
    return turned.reshape(row_count, -1).astype(jnp.bfloat16)

def segment_info(lengths, first_row, row_count):
    request_end = jnp.cumsum(lengths).astype(jnp.int32)
    request_start = (request_end - lengths).astype(jnp.int32)
    global_row = (first_row + jnp.arange(row_count, dtype=jnp.int32)).astype(jnp.int32)
    segment = lax.optimization_barrier(jnp.sum((request_end[None, :] <= global_row[:, None]).astype(jnp.int32), axis=1)).astype(jnp.int32)
    chosen = segment[:, None] == jnp.arange(lengths.shape[0], dtype=jnp.int32)[None, :]
    begin = lax.optimization_barrier(jnp.sum(jnp.where(chosen, request_start[None, :], 0), axis=1)).astype(jnp.int32)
    return (segment, (global_row - begin).astype(jnp.int32), global_row)

def reference(tokens, lengths, keep_mask, routes, attention_gain, mixture_gain, query_gain, key_gain, query_weight, key_weight, value_weight, output_weight, router_weight, expert_gate, expert_up, expert_down):
    xfloat = tokens.astype(jnp.float32)
    normed_in = (xfloat * lax.rsqrt(lax.optimization_barrier(jnp.mean(xfloat * xfloat, axis=1, keepdims=True)) + EPS) * attention_gain).astype(jnp.bfloat16)
    segment, position, global_row = segment_info(lengths, 0, TOKENS)
    cos_table, sin_table = rope_tables(position)
    queries = head_prep(jnp.dot(normed_in, query_weight, preferred_element_type=jnp.float32), query_gain, cos_table, sin_table)
    key_heads = head_prep(jnp.dot(normed_in, key_weight, preferred_element_type=jnp.float32), key_gain, cos_table, sin_table)
    value_heads = jnp.dot(normed_in, value_weight, preferred_element_type=jnp.float32).astype(jnp.bfloat16)
    qblock = math.gcd(TOKENS, 512)
    blocks = TOKENS // qblock
    query_blocks = queries.reshape(blocks, qblock, HEADS, HEAD_DIM)
    key_float = key_heads.reshape(TOKENS, HEADS, HEAD_DIM).astype(jnp.float32)
    value_float = value_heads.reshape(TOKENS, HEADS, HEAD_DIM).astype(jnp.float32)
    scale = HEAD_DIM ** (-0.5)

    def attend(packed):
        query_part, query_seg, query_row = packed
        scores = jnp.einsum('thd,shd->hts', query_part.astype(jnp.float32), key_float) * scale
        visible = (query_seg[:, None] == segment[None, :]) & ((keep_mask[None, :] == 1) | (query_row[:, None] == global_row[None, :]))
        masked = jnp.where(visible[None], scores, NEG)
        top_score = lax.optimization_barrier(jnp.max(masked, axis=2, keepdims=True))
        weights = jnp.where(visible[None], jnp.exp(masked - top_score), 0.0)
        totals = lax.optimization_barrier(jnp.sum(weights, axis=2))
        rounded = lax.optimization_barrier(weights.astype(jnp.bfloat16))
        mixed = jnp.einsum('hts,shd->thd', rounded.astype(jnp.float32), value_float)
        return (mixed / totals.T[:, :, None]).reshape(qblock, D).astype(jnp.bfloat16)
    attended = lax.map(attend, (query_blocks, segment.reshape(blocks, qblock), global_row.reshape(blocks, qblock))).reshape(TOKENS, D)
    residual = (xfloat + jnp.dot(attended, output_weight, preferred_element_type=jnp.float32)).astype(jnp.bfloat16)
    hfloat = residual.astype(jnp.float32)
    inverse = lax.rsqrt(lax.optimization_barrier(jnp.mean(hfloat * hfloat, axis=1, keepdims=True)) + EPS)
    scaled = hfloat * mixture_gain
    mixed_in = (scaled * inverse).astype(jnp.bfloat16)
    logits = jnp.dot(scaled, router_weight, precision=lax.Precision.HIGHEST) * inverse
    picked = jnp.take_along_axis(logits, routes, axis=1)
    sigmoid_vals = jax.nn.sigmoid(picked)
    route_weight = sigmoid_vals / lax.optimization_barrier(jnp.sum(sigmoid_vals, axis=1, keepdims=True))
    onehot = lax.optimization_barrier(jnp.sum((routes[:, :, None] == jnp.arange(EXPERTS, dtype=jnp.int32)[None, None, :]).astype(jnp.int32), axis=1)).astype(jnp.int32)
    per_block = onehot.reshape(N_DP, TOK_DEV, EXPERTS)
    before = (jnp.cumsum(per_block, axis=1).astype(jnp.int32) - per_block).reshape(TOKENS, EXPERTS)
    slot = jnp.take_along_axis(before, routes, axis=1).astype(jnp.int32)
    block_id = (jnp.arange(TOKENS, dtype=jnp.int32) // TOK_DEV)[:, None]
    target = (routes * (N_DP * CAP) + block_id * CAP + slot).astype(jnp.int32)
    token_ids = jnp.repeat(jnp.arange(TOKENS, dtype=jnp.int32), TOPK)
    source = jnp.full((EXPERTS * N_DP * CAP,), TOKENS, jnp.int32).at[target.reshape(-1)].set(token_ids)
    padded = jnp.concatenate([mixed_in, jnp.zeros((1, D), jnp.bfloat16)], 0)
    gate_all = expert_gate.reshape(N_DP, D, EXP_DEV, FF).transpose(0, 2, 1, 3).reshape(EXPERTS, D, FF)
    up_all = expert_up.reshape(N_DP, D, EXP_DEV, FF).transpose(0, 2, 1, 3).reshape(EXPERTS, D, FF)
    down_all = expert_down.reshape(EXPERTS, FF, D)
    ff_block = FF // SPLIT

    def expert_ffn(packed):
        row_index, gate_w, up_w, down_w = packed
        inputs = padded[row_index]
        gate_val = jnp.dot(inputs, gate_w, preferred_element_type=jnp.float32)
        up_val = jnp.dot(inputs, up_w, preferred_element_type=jnp.float32)
        hidden = (jax.nn.silu(gate_val) * up_val).astype(jnp.bfloat16)
        row_count = hidden.shape[0]
        partial_value = jnp.einsum('rjf,jfd->rjd', hidden.reshape(row_count, SPLIT, ff_block).astype(jnp.float32), down_w.reshape(SPLIT, ff_block, D).astype(jnp.float32))
        rounded = lax.optimization_barrier(partial_value.astype(jnp.bfloat16))
        return lax.optimization_barrier(jnp.sum(rounded.astype(jnp.float32), axis=1)).astype(jnp.bfloat16)
    expert_out = lax.map(expert_ffn, (source.reshape(EXPERTS, N_DP * CAP), gate_all, up_all, down_all))
    flat = expert_out.reshape(EXPERTS * N_DP * CAP, D)
    gathered = flat[target]
    mixture = lax.optimization_barrier(jnp.sum(gathered.astype(jnp.float32) * route_weight[:, :, None], axis=1))
    return (hfloat + mixture).astype(jnp.bfloat16)
```

```python
import jax
import jax.numpy as jnp
from jax import lax
from jax.sharding import PartitionSpec as P

D = 2048
HEAD_DIM = 128
FF = 1024
EXPERTS = 64
TOPK = 8
CAP = 32


EPS = 1e-06
ROPE_BASE = 10000.0
NEG = -1e30


def rope_tables(position):
    halves = HEAD_DIM // 2
    exponent = jnp.arange(halves, dtype=jnp.float32) * (2.0 / HEAD_DIM)
    frequency = jnp.power(jnp.float32(ROPE_BASE), -exponent)
    angle = position.astype(jnp.float32)[:, None] * frequency[None, :]
    cos_table = jnp.cos(angle)
    sin_table = jnp.sin(angle)
    return (jnp.concatenate([cos_table, cos_table], 1), jnp.concatenate([sin_table, sin_table], 1))


def head_prep(projected, head_gain, cos_table, sin_table):
    row_count = projected.shape[0]
    per_head = projected.reshape(row_count, -1, HEAD_DIM)
    normed = (
        per_head * lax.rsqrt(jnp.mean(per_head * per_head, axis=2, keepdims=True) + EPS) * head_gain
    )
    halves = HEAD_DIM // 2
    rotated = jnp.concatenate([-normed[:, :, halves:], normed[:, :, :halves]], 2)
    turned = normed * cos_table[:, None, :] + rotated * sin_table[:, None, :]
    return turned.reshape(row_count, -1).astype(jnp.bfloat16)


def segment_info(lengths, global_row):
    request_end = jnp.cumsum(lengths)
    request_start = request_end - lengths
    segment = jnp.sum((request_end[None, :] <= global_row[:, None]).astype(jnp.int32), axis=1)
    chosen = segment[:, None] == jnp.arange(lengths.shape[0], dtype=jnp.int32)[None, :]
    begin = jnp.sum(jnp.where(chosen, request_start[None, :], 0), axis=1)
    return (segment, global_row - begin)


def gather_tokens(block):
    return lax.all_gather(block, "dp", axis=0, tiled=True)


def attention(queries, keys, values, query_seg, query_row, key_seg, key_row, keep_mask):
    scale = HEAD_DIM ** (-0.5)
    scores = (
        lax.dot_general(
            queries, keys, (((1,), (1,)), ((), ())), preferred_element_type=jnp.float32
        )
        * scale
    )
    visible = (query_seg[:, None] == key_seg[None, :]) & (
        (keep_mask[None, :] == 1) | (query_row[:, None] == key_row[None, :])
    )
    masked = jnp.where(visible, scores, NEG)
    top = jnp.max(masked, axis=1, keepdims=True)
    weights = jnp.where(visible, jnp.exp(masked - top), 0.0)
    totals = jnp.sum(weights, axis=1, keepdims=True)
    mixed = jnp.dot(weights.astype(jnp.bfloat16), values, preferred_element_type=jnp.float32)
    return (mixed / totals).astype(jnp.bfloat16)


def local(
    tokens,
    lengths,
    keep_mask,
    routes,
    attention_gain,
    mixture_gain,
    query_gain,
    key_gain,
    query_weight,
    key_weight,
    value_weight,
    output_weight,
    router_weight,
    expert_gate,
    expert_up,
    expert_down,
):
    tok_rows = tokens.shape[0]
    dp_count = lax.axis_size("dp")
    dp_index = lax.axis_index("dp")
    mp_index = lax.axis_index("mp")
    local_width = query_weight.shape[1]
    local_heads = local_width // HEAD_DIM
    share = dp_count // local_heads
    part = dp_index % share
    total_rows = tok_rows * dp_count

    weight_rows = query_weight.shape[0]
    packed = jnp.stack([query_weight, key_weight, value_weight]).reshape(
        3, weight_rows, local_heads, HEAD_DIM
    )
    packed = packed.transpose(2, 1, 0, 3).reshape(local_heads, weight_rows, 3 * HEAD_DIM)
    packed = jnp.repeat(packed, share, axis=0)
    head_weight = lax.all_to_all(packed, "dp", split_axis=0, concat_axis=0, tiled=True)
    head_weight = head_weight.reshape(dp_count * weight_rows, 3 * HEAD_DIM)

    full_tokens = lax.all_gather(tokens, "mp", axis=1, tiled=True)
    xfloat = full_tokens.astype(jnp.float32)
    normed_in = (
        xfloat * lax.rsqrt(jnp.mean(xfloat * xfloat, axis=1, keepdims=True) + EPS) * attention_gain
    ).astype(jnp.bfloat16)
    all_in = gather_tokens(normed_in)
    all_output_weight = lax.all_gather(output_weight, "dp", axis=1, tiled=True)

    key_row = jnp.arange(total_rows, dtype=jnp.int32)
    key_seg, key_pos = segment_info(lengths, key_row)
    cos_table, sin_table = rope_tables(key_pos)

    def own(array):
        split = array.reshape((local_heads, share, tok_rows) + array.shape[1:])
        taken = lax.dynamic_index_in_dim(split, part, 1, keepdims=False)
        return taken.reshape((local_heads * tok_rows,) + array.shape[1:])

    projected = jnp.dot(all_in, head_weight, preferred_element_type=jnp.float32)
    queries = head_prep(
        own(projected[:, :HEAD_DIM]), query_gain, own(cos_table), own(sin_table)
    )
    keys = head_prep(projected[:, HEAD_DIM : 2 * HEAD_DIM], key_gain, cos_table, sin_table)
    values = projected[:, 2 * HEAD_DIM :].astype(jnp.bfloat16)
    attended = attention(
        queries, keys, values, own(key_seg), own(key_row), key_seg, key_row, keep_mask
    )
    groups = [[head * share + p for head in range(local_heads)] for p in range(share)]
    attended = lax.all_to_all(
        attended.reshape(local_heads, tok_rows, HEAD_DIM),
        "dp",
        split_axis=0,
        concat_axis=0,
        tiled=True,
        axis_index_groups=groups,
    )
    attended = attended.transpose(1, 0, 2).reshape(tok_rows, local_width)
    partial_out = jnp.dot(attended, all_output_weight, preferred_element_type=jnp.float32)
    summed_out = lax.psum_scatter(partial_out, "mp", scatter_dimension=1, tiled=True)
    residual = (tokens.astype(jnp.float32) + summed_out).astype(jnp.bfloat16)
    hfloat = residual.astype(jnp.float32)
    scaled = hfloat * mixture_gain
    partial_logits = jnp.dot(scaled, router_weight, precision=lax.Precision.HIGHEST)
    square_sum, logit_sum = lax.psum((jnp.sum(hfloat * hfloat, axis=1), partial_logits), "mp")
    inverse = lax.rsqrt(square_sum / D + EPS)[:, None]
    mixed_in = (scaled * inverse).astype(jnp.bfloat16)
    logits = logit_sum * inverse

    experts = jnp.arange(EXPERTS, dtype=jnp.int32)
    named = jnp.any(routes[None, :, :] == experts[:, None, None], axis=2)
    named_float = named.astype(jnp.float32)
    sigmoid_vals = jax.nn.sigmoid(logits).T * named_float
    route_weight = sigmoid_vals / jnp.sum(sigmoid_vals, axis=0, keepdims=True)
    ids = jnp.arange(tok_rows, dtype=jnp.int32)
    earlier = (ids[:, None] < ids[None, :]).astype(jnp.bfloat16)
    before = jnp.dot(named.astype(jnp.bfloat16), earlier, preferred_element_type=jnp.float32)
    place = jnp.where(named, before.astype(jnp.int32), -1)

    exp_local = EXPERTS // dp_count
    gate_local = expert_gate[0]
    up_local = expert_up[0]
    down_local = expert_down[0]
    unit_count = gate_local.shape[1]
    held = max(1, unit_count // FF)
    units = unit_count // held
    first_expert = (mp_index * unit_count) // FF

    def mine(table):
        split = table.reshape(dp_count, exp_local, tok_rows)
        return lax.dynamic_slice_in_dim(split, first_expert, held, 1)

    slots = jnp.arange(CAP, dtype=jnp.int32)
    chosen = mine(place)[:, :, None, :] == slots[None, None, :, None]
    select = chosen.astype(jnp.bfloat16).reshape(dp_count * held * CAP, tok_rows)
    full_in = lax.all_gather(mixed_in, "mp", axis=1, tiled=True)
    sending = jnp.dot(select, full_in, preferred_element_type=jnp.float32).astype(jnp.bfloat16)
    rows_in = lax.all_to_all(
        sending.reshape(dp_count, held, CAP, D), "dp", split_axis=0, concat_axis=0, tiled=True
    )
    outs = []
    for index in range(held):
        rows = rows_in[:, index].reshape(dp_count * CAP, D)
        low, high = index * units, (index + 1) * units
        gate_val = jnp.dot(rows, gate_local[:, low:high], preferred_element_type=jnp.float32)
        up_val = jnp.dot(rows, up_local[:, low:high], preferred_element_type=jnp.float32)
        hidden = (jax.nn.silu(gate_val) * up_val).astype(jnp.bfloat16)
        out = jnp.dot(hidden, down_local[low:high], preferred_element_type=jnp.float32)
        outs.append(out.astype(jnp.bfloat16).reshape(dp_count, CAP, D))
    returned = lax.all_to_all(
        jnp.stack(outs, axis=1), "dp", split_axis=0, concat_axis=0, tiled=True
    ).reshape(dp_count * held * CAP, D)
    spread = jnp.where(chosen, mine(route_weight)[:, :, None, :], 0.0)
    spread = spread.reshape(dp_count * held * CAP, tok_rows)
    spread_high = spread.astype(jnp.bfloat16)
    spread_mid = (spread - spread_high.astype(jnp.float32)).astype(jnp.bfloat16)
    contract = (((0,), (0,)), ((), ()))
    mixture = lax.dot_general(
        spread_high, returned, contract, preferred_element_type=jnp.float32
    ) + lax.dot_general(spread_mid, returned, contract, preferred_element_type=jnp.float32)
    mixture = lax.psum_scatter(mixture, "mp", scatter_dimension=1, tiled=True)
    return (hfloat + mixture).astype(jnp.bfloat16)


def solution(mesh):
    return jax.shard_map(
        local,
        mesh=mesh,
        in_specs=(
            P("dp", "mp"),
            P(),
            P(),
            P("dp", None),
            P(),
            P("mp"),
            P(),
            P(),
            P("dp", "mp"),
            P("dp", "mp"),
            P("dp", "mp"),
            P("mp", "dp"),
            P("mp", None),
            P("dp", None, "mp"),
            P("dp", None, "mp"),
            P("dp", "mp", None),
        ),
        out_specs=P("dp", "mp"),
        check_vma=False,
    )
```

```python
import jax
import jax.numpy as jnp
from jax import lax
from jax.experimental import pallas as pl
from jax.experimental.pallas import tpu as pltpu
from jax.sharding import PartitionSpec as P

D = 2048
HEAD_DIM = 128
FF = 1024
EXPERTS = 64
TOPK = 8
CAP = 32


EPS = 1e-06
ROPE_BASE = 10000.0
NEG = -1e30


def rope_tables(position):
    halves = HEAD_DIM // 2
    exponent = jnp.arange(halves, dtype=jnp.float32) * (2.0 / HEAD_DIM)
    frequency = jnp.power(jnp.float32(ROPE_BASE), -exponent)
    angle = position.astype(jnp.float32)[:, None] * frequency[None, :]
    cos_table = jnp.cos(angle)
    sin_table = jnp.sin(angle)
    return (jnp.concatenate([cos_table, cos_table], 1), jnp.concatenate([sin_table, sin_table], 1))


def head_prep(projected, head_gain, cos_table, sin_table):
    row_count = projected.shape[0]
    per_head = projected.reshape(row_count, -1, HEAD_DIM)
    normed = (
        per_head * lax.rsqrt(jnp.mean(per_head * per_head, axis=2, keepdims=True) + EPS) * head_gain
    )
    halves = HEAD_DIM // 2
    rotated = jnp.concatenate([-normed[:, :, halves:], normed[:, :, :halves]], 2)
    turned = normed * cos_table[:, None, :] + rotated * sin_table[:, None, :]
    return turned.reshape(row_count, -1).astype(jnp.bfloat16)


def segment_info(lengths, global_row):
    request_end = jnp.cumsum(lengths)
    request_start = request_end - lengths
    segment = jnp.sum((request_end[None, :] <= global_row[:, None]).astype(jnp.int32), axis=1)
    chosen = segment[:, None] == jnp.arange(lengths.shape[0], dtype=jnp.int32)[None, :]
    begin = jnp.sum(jnp.where(chosen, request_start[None, :], 0), axis=1)
    return (segment, global_row - begin)


MESH = pl.DeviceIdType.MESH


def gather_kernel(block_ref, out_ref, local_sem, a_sem, up_sem, down_sem, b_sem, twin_sem, recv_sem):
    index = lax.axis_index("dp")
    x = lax.axis_index("mp")
    layers = lax.axis_size("dp") // 4
    z, y, core = index // 4, (index // 2) % 2, index % 2
    rows, width = block_ref.shape
    to_a = (index + core * (2 - 4 * y), x + (1 - core) * (1 - 2 * x))
    to_b = (index + (1 - core) * (2 - 4 * y), x + core * (1 - 2 * x))
    to_twin = (index + 1 - 2 * core, x)
    to_up, to_down = (index + 4, x), (index - 4, x)

    def place(layer, da, db, which):
        dy = which * da + (1 - which) * db
        dx = (1 - which) * da + which * db
        yy, xx = y + dy * (1 - 2 * y), x + dx * (1 - 2 * x)
        return layer * 4 + yy * 2 + which, xx

    def view(spot):
        return out_ref.at[
            pl.ds(pl.multiple_of(spot[0] * rows, rows), rows),
            pl.ds(pl.multiple_of(spot[1] * width, width), width),
        ]

    def send(spot, sem, device, own=False):
        return pltpu.make_async_remote_copy(
            src_ref=block_ref if own else view(spot),
            dst_ref=view(spot),
            send_sem=sem,
            recv_sem=recv_sem.at[spot[0] * 2 + spot[1]],
            device_id=device,
            device_id_type=MESH,
        )

    def arrive(spot):
        send(spot, local_sem, to_twin).wait_recv()

    barrier = pltpu.get_barrier_semaphore()
    for peer in (to_a, to_b, to_twin):
        pl.semaphore_signal(barrier, inc=1, device_id=peer, device_id_type=MESH)
    has_up, has_down = z < layers - 1, z > 0

    @pl.when(has_up)
    def _():
        pl.semaphore_signal(barrier, inc=1, device_id=to_up, device_id_type=MESH)

    @pl.when(has_down)
    def _():
        pl.semaphore_signal(barrier, inc=1, device_id=to_down, device_id_type=MESH)

    pl.semaphore_wait(
        barrier, 3 + has_up.astype(jnp.int32) + has_down.astype(jnp.int32)
    )

    home = place(z, 0, 0, core)
    keep = pltpu.make_async_copy(block_ref, view(home), local_sem)
    first = send(home, a_sem, to_a, True)

    def spread(layer, da, own, act):
        spot = place(layer, da, 0, core)
        slot = layer * 2 + da

        @pl.when((layer <= z) & has_up)
        def _():
            act(send(spot, up_sem.at[slot], to_up, own))

        @pl.when((layer >= z) & has_down)
        def _():
            act(send(spot, down_sem.at[slot], to_down, own))

        act(send(spot, b_sem.at[slot], to_b, own))
        act(send(spot, twin_sem.at[slot * 2], to_twin, own))

    def hand_over(layer, da, act):
        spot = place(layer, da, 1, core)
        act(send(spot, twin_sem.at[(layer * 2 + da) * 2 + 1], to_twin))

    start = lambda copy: copy.start()
    finish = lambda copy: copy.wait_send()
    first.start()
    spread(z, 0, True, start)
    keep.start()
    arrive(place(z, 1, 0, core))
    spread(z, 1, False, start)

    def both(distance, run):
        for da in range(2):
            @pl.when(z >= distance)
            def _():
                run(z - distance, da)

            @pl.when(z + distance < layers)
            def _():
                run(z + distance, da)

    def onward(layer, da):
        arrive(place(layer, da, 0, core))
        spread(layer, da, False, start)

    def across(layer, da):
        arrive(place(layer, da, 1, core))
        hand_over(layer, da, start)

    for distance in range(1, layers):
        both(distance, onward)
        if distance == 1:
            for da in range(2):
                across(z, da)
        else:
            both(distance - 1, across)
    both(layers - 1, across)
    keep.wait()
    first.wait_send()
    for layer in range(layers):
        for da in range(2):
            spread(layer, da, False, finish)
            hand_over(layer, da, finish)
            for db in range(2):
                arrive(place(layer, da, db, 1 - core))


def gather_blocks(block):
    dp_count, mp_count = lax.axis_size("dp"), lax.axis_size("mp")
    rows, width = block.shape
    if mp_count != 2 or dp_count % 4:
        wide = lax.all_gather(block, "mp", axis=1, tiled=True)
        return lax.all_gather(wide, "dp", axis=0, tiled=True)
    layers = dp_count // 4
    dma = pltpu.SemaphoreType.DMA
    return pl.pallas_call(
        gather_kernel,
        out_shape=jax.ShapeDtypeStruct((dp_count * rows, mp_count * width), block.dtype),
        in_specs=[pl.BlockSpec(memory_space=pl.ANY)],
        out_specs=pl.BlockSpec(memory_space=pl.ANY),
        scratch_shapes=[
            dma,
            dma,
            dma((layers * 2,)),
            dma((layers * 2,)),
            dma((layers * 2,)),
            dma((layers * 4,)),
            dma((dp_count * mp_count,)),
        ],
        compiler_params=pltpu.CompilerParams(collective_id=0, has_side_effects=True),
        name="gather_blocks",
    )(block)


def attention(queries, keys, values, query_seg, query_row, key_seg, key_row, keep_mask):
    scale = HEAD_DIM ** (-0.5)
    scores = (
        lax.dot_general(
            queries, keys, (((1,), (1,)), ((), ())), preferred_element_type=jnp.float32
        )
        * scale
    )
    visible = (query_seg[:, None] == key_seg[None, :]) & (
        (keep_mask[None, :] == 1) | (query_row[:, None] == key_row[None, :])
    )
    masked = jnp.where(visible, scores, NEG)
    top = jnp.max(masked, axis=1, keepdims=True)
    weights = jnp.where(visible, jnp.exp(masked - top), 0.0)
    totals = jnp.sum(weights, axis=1, keepdims=True)
    mixed = jnp.dot(weights.astype(jnp.bfloat16), values, preferred_element_type=jnp.float32)
    return (mixed / totals).astype(jnp.bfloat16)


def local(
    tokens,
    lengths,
    keep_mask,
    routes,
    attention_gain,
    mixture_gain,
    query_gain,
    key_gain,
    query_weight,
    key_weight,
    value_weight,
    output_weight,
    router_weight,
    expert_gate,
    expert_up,
    expert_down,
):
    tok_rows = tokens.shape[0]
    dp_count = lax.axis_size("dp")
    dp_index = lax.axis_index("dp")
    mp_index = lax.axis_index("mp")
    local_width = query_weight.shape[1]
    local_heads = local_width // HEAD_DIM
    share = dp_count // local_heads
    part = dp_index % share
    total_rows = tok_rows * dp_count

    weight_rows = query_weight.shape[0]
    packed = jnp.stack([query_weight, key_weight, value_weight]).reshape(
        3, weight_rows, local_heads, HEAD_DIM
    )
    packed = packed.transpose(2, 1, 0, 3).reshape(local_heads, weight_rows, 3 * HEAD_DIM)
    packed = jnp.repeat(packed, share, axis=0)
    head_weight = lax.all_to_all(packed, "dp", split_axis=0, concat_axis=0, tiled=True)
    head_weight = head_weight.reshape(dp_count * weight_rows, 3 * HEAD_DIM)

    all_tokens = gather_blocks(tokens)
    xfloat = all_tokens.astype(jnp.float32)
    all_in = (
        xfloat * lax.rsqrt(jnp.mean(xfloat * xfloat, axis=1, keepdims=True) + EPS) * attention_gain
    ).astype(jnp.bfloat16)
    all_routes = lax.all_gather(routes, "dp", axis=0, tiled=True)
    all_gain = lax.all_gather(mixture_gain, "mp", axis=0, tiled=True)
    all_router = lax.all_gather(router_weight, "mp", axis=0, tiled=True)
    all_output_weight = lax.all_gather(output_weight, "dp", axis=1, tiled=True)

    key_row = jnp.arange(total_rows, dtype=jnp.int32)
    key_seg, key_pos = segment_info(lengths, key_row)
    cos_table, sin_table = rope_tables(key_pos)

    def own(array):
        split = array.reshape((local_heads, share, tok_rows) + array.shape[1:])
        taken = lax.dynamic_index_in_dim(split, part, 1, keepdims=False)
        return taken.reshape((local_heads * tok_rows,) + array.shape[1:])

    projected = jnp.dot(all_in, head_weight, preferred_element_type=jnp.float32)
    queries = head_prep(
        own(projected[:, :HEAD_DIM]), query_gain, own(cos_table), own(sin_table)
    )
    keys = head_prep(projected[:, HEAD_DIM : 2 * HEAD_DIM], key_gain, cos_table, sin_table)
    values = projected[:, 2 * HEAD_DIM :].astype(jnp.bfloat16)
    attended = attention(
        queries, keys, values, own(key_seg), own(key_row), key_seg, key_row, keep_mask
    )
    groups = [[head * share + p for head in range(local_heads)] for p in range(share)]
    attended = lax.all_to_all(
        attended.reshape(local_heads, tok_rows, HEAD_DIM),
        "dp",
        split_axis=0,
        concat_axis=0,
        tiled=True,
        axis_index_groups=groups,
    )
    attended = attended.transpose(1, 0, 2).reshape(tok_rows, local_width)
    partial_out = jnp.dot(attended, all_output_weight, preferred_element_type=jnp.float32)
    summed_out = lax.psum_scatter(partial_out, "mp", scatter_dimension=1, tiled=True)
    residual = (tokens.astype(jnp.float32) + summed_out).astype(jnp.bfloat16)
    all_residual = gather_blocks(residual)
    hfloat = all_residual.astype(jnp.float32)
    inverse = lax.rsqrt(jnp.mean(hfloat * hfloat, axis=1, keepdims=True) + EPS)
    mixed_in = (hfloat * all_gain * inverse).astype(jnp.bfloat16)

    own_rows = lax.dynamic_slice_in_dim(all_residual, dp_index * tok_rows, tok_rows, 0)
    own_float = own_rows.astype(jnp.float32)
    own_inverse = lax.rsqrt(jnp.mean(own_float * own_float, axis=1, keepdims=True) + EPS)
    logits = (
        jnp.dot(own_float * all_gain, all_router, precision=lax.Precision.HIGHEST) * own_inverse
    )

    ids = jnp.arange(tok_rows, dtype=jnp.int32)
    earlier = (ids[:, None] < ids[None, :]).astype(jnp.bfloat16)
    slots = jnp.arange(CAP, dtype=jnp.int32)

    def chosen_slots(named):
        before = jnp.dot(
            named.astype(jnp.bfloat16).reshape(-1, tok_rows),
            earlier,
            preferred_element_type=jnp.float32,
        ).reshape(named.shape)
        place = jnp.where(named, before.astype(jnp.int32), -1)
        return place[:, :, None, :] == slots[None, None, :, None]

    exp_local = EXPERTS // dp_count
    gate_local = expert_gate[0]
    up_local = expert_up[0]
    down_local = expert_down[0]
    unit_count = gate_local.shape[1]
    held = max(1, unit_count // FF)
    units = unit_count // held
    first_expert = (mp_index * unit_count) // FF

    own_experts = dp_index * exp_local + first_expert + jnp.arange(held, dtype=jnp.int32)
    block_routes = all_routes.reshape(dp_count, tok_rows, TOPK)
    here = jnp.any(block_routes[:, None] == own_experts[None, :, None, None], axis=3)
    select = chosen_slots(here).astype(jnp.bfloat16).reshape(dp_count, held * CAP, tok_rows)
    rows_in = lax.dot_general(
        select,
        mixed_in.reshape(dp_count, tok_rows, D),
        (((2,), (1,)), ((0,), (0,))),
        preferred_element_type=jnp.float32,
    ).astype(jnp.bfloat16)
    rows_in = rows_in.reshape(dp_count, held, CAP, D)
    outs = []
    for index in range(held):
        rows = rows_in[:, index].reshape(dp_count * CAP, D)
        low, high = index * units, (index + 1) * units
        gate_val = jnp.dot(rows, gate_local[:, low:high], preferred_element_type=jnp.float32)
        up_val = jnp.dot(rows, up_local[:, low:high], preferred_element_type=jnp.float32)
        hidden = (jax.nn.silu(gate_val) * up_val).astype(jnp.bfloat16)
        out = jnp.dot(hidden, down_local[low:high], preferred_element_type=jnp.float32)
        outs.append(out.astype(jnp.bfloat16).reshape(dp_count, CAP, D))
    returned = lax.all_to_all(
        jnp.stack(outs, axis=1), "dp", split_axis=0, concat_axis=0, tiled=True
    ).reshape(dp_count * held * CAP, D)
    experts = jnp.arange(EXPERTS, dtype=jnp.int32)
    named = jnp.any(routes[None, :, :] == experts[:, None, None], axis=2)
    sigmoid_vals = jax.nn.sigmoid(logits).T * named.astype(jnp.float32)
    route_weight = sigmoid_vals / jnp.sum(sigmoid_vals, axis=0, keepdims=True)

    def mine(table):
        split = table.reshape(dp_count, exp_local, tok_rows)
        return lax.dynamic_slice_in_dim(split, first_expert, held, 1)

    spread = jnp.where(chosen_slots(mine(named)), mine(route_weight)[:, :, None, :], 0.0)
    spread = spread.reshape(dp_count * held * CAP, tok_rows)
    spread_high = spread.astype(jnp.bfloat16)
    spread_mid = (spread - spread_high.astype(jnp.float32)).astype(jnp.bfloat16)
    contract = (((0,), (0,)), ((), ()))
    mixture = lax.dot_general(
        spread_high, returned, contract, preferred_element_type=jnp.float32
    ) + lax.dot_general(spread_mid, returned, contract, preferred_element_type=jnp.float32)
    mixture = lax.psum_scatter(mixture, "mp", scatter_dimension=1, tiled=True)
    return (residual.astype(jnp.float32) + mixture).astype(jnp.bfloat16)


def solution(mesh):
    return jax.shard_map(
        local,
        mesh=mesh,
        in_specs=(
            P("dp", "mp"),
            P(),
            P(),
            P("dp", None),
            P(),
            P("mp"),
            P(),
            P(),
            P("dp", "mp"),
            P("dp", "mp"),
            P("dp", "mp"),
            P("mp", "dp"),
            P("mp", None),
            P("dp", None, "mp"),
            P("dp", None, "mp"),
            P("dp", "mp", None),
        ),
        out_specs=P("dp", "mp"),
        check_vma=False,
    )
```

```python
import jax
import jax.numpy as jnp
from jax import lax
from jax.experimental import pallas as pl
from jax.experimental.pallas import tpu as pltpu
from jax.sharding import PartitionSpec as P

D = 2048
HEAD_DIM = 128
FF = 1024
EXPERTS = 64
TOPK = 8
CAP = 32


EPS = 1e-06
ROPE_BASE = 10000.0
NEG = -1e30


def rope_tables(position):
    halves = HEAD_DIM // 2
    exponent = jnp.arange(halves, dtype=jnp.float32) * (2.0 / HEAD_DIM)
    frequency = jnp.power(jnp.float32(ROPE_BASE), -exponent)
    angle = position.astype(jnp.float32)[:, None] * frequency[None, :]
    cos_table = jnp.cos(angle)
    sin_table = jnp.sin(angle)
    return (jnp.concatenate([cos_table, cos_table], 1), jnp.concatenate([sin_table, sin_table], 1))


def head_prep(projected, head_gain, cos_table, sin_table):
    row_count = projected.shape[0]
    per_head = projected.reshape(row_count, -1, HEAD_DIM)
    normed = (
        per_head * lax.rsqrt(jnp.mean(per_head * per_head, axis=2, keepdims=True) + EPS) * head_gain
    )
    halves = HEAD_DIM // 2
    rotated = jnp.concatenate([-normed[:, :, halves:], normed[:, :, :halves]], 2)
    turned = normed * cos_table[:, None, :] + rotated * sin_table[:, None, :]
    return turned.reshape(row_count, -1).astype(jnp.bfloat16)


def segment_info(lengths, global_row):
    request_end = jnp.cumsum(lengths)
    request_start = request_end - lengths
    segment = jnp.sum((request_end[None, :] <= global_row[:, None]).astype(jnp.int32), axis=1)
    chosen = segment[:, None] == jnp.arange(lengths.shape[0], dtype=jnp.int32)[None, :]
    begin = jnp.sum(jnp.where(chosen, request_start[None, :], 0), axis=1)
    return (segment, global_row - begin)


MESH = pl.DeviceIdType.MESH


def gather_kernel(block_ref, out_ref, local_sem, a_sem, up_sem, down_sem, b_sem, twin_sem, recv_sem):
    index = lax.axis_index("dp")
    x = lax.axis_index("mp")
    layers = lax.axis_size("dp") // 4
    z, y, core = index // 4, (index // 2) % 2, index % 2
    rows, width = block_ref.shape
    to_a = (index + core * (2 - 4 * y), x + (1 - core) * (1 - 2 * x))
    to_b = (index + (1 - core) * (2 - 4 * y), x + core * (1 - 2 * x))
    to_twin = (index + 1 - 2 * core, x)
    to_up, to_down = (index + 4, x), (index - 4, x)

    def place(layer, da, db, which):
        dy = which * da + (1 - which) * db
        dx = (1 - which) * da + which * db
        yy, xx = y + dy * (1 - 2 * y), x + dx * (1 - 2 * x)
        return layer * 4 + yy * 2 + which, xx

    def view(spot):
        return out_ref.at[
            pl.ds(pl.multiple_of(spot[0] * rows, rows), rows),
            pl.ds(pl.multiple_of(spot[1] * width, width), width),
        ]

    def send(spot, sem, device, own=False):
        return pltpu.make_async_remote_copy(
            src_ref=block_ref if own else view(spot),
            dst_ref=view(spot),
            send_sem=sem,
            recv_sem=recv_sem.at[spot[0] * 2 + spot[1]],
            device_id=device,
            device_id_type=MESH,
        )

    def arrive(spot):
        send(spot, local_sem, to_twin).wait_recv()

    barrier = pltpu.get_barrier_semaphore()
    for peer in (to_a, to_b, to_twin):
        pl.semaphore_signal(barrier, inc=1, device_id=peer, device_id_type=MESH)
    has_up, has_down = z < layers - 1, z > 0

    @pl.when(has_up)
    def _():
        pl.semaphore_signal(barrier, inc=1, device_id=to_up, device_id_type=MESH)

    @pl.when(has_down)
    def _():
        pl.semaphore_signal(barrier, inc=1, device_id=to_down, device_id_type=MESH)

    pl.semaphore_wait(
        barrier, 3 + has_up.astype(jnp.int32) + has_down.astype(jnp.int32)
    )

    home = place(z, 0, 0, core)
    keep = pltpu.make_async_copy(block_ref, view(home), local_sem)
    first = send(home, a_sem, to_a, True)

    def spread(layer, da, own, act):
        spot = place(layer, da, 0, core)
        slot = layer * 2 + da

        @pl.when((layer <= z) & has_up)
        def _():
            act(send(spot, up_sem.at[slot], to_up, own))

        @pl.when((layer >= z) & has_down)
        def _():
            act(send(spot, down_sem.at[slot], to_down, own))

        act(send(spot, b_sem.at[slot], to_b, own))
        act(send(spot, twin_sem.at[slot * 2], to_twin, own))

    def hand_over(layer, da, act):
        spot = place(layer, da, 1, core)
        act(send(spot, twin_sem.at[(layer * 2 + da) * 2 + 1], to_twin))

    start = lambda copy: copy.start()
    finish = lambda copy: copy.wait_send()
    first.start()
    spread(z, 0, True, start)
    keep.start()
    arrive(place(z, 1, 0, core))
    spread(z, 1, False, start)

    def both(distance, run):
        for da in range(2):
            @pl.when(z >= distance)
            def _():
                run(z - distance, da)

            @pl.when(z + distance < layers)
            def _():
                run(z + distance, da)

    def onward(layer, da):
        arrive(place(layer, da, 0, core))
        spread(layer, da, False, start)

    def across(layer, da):
        arrive(place(layer, da, 1, core))
        hand_over(layer, da, start)

    for distance in range(1, layers):
        both(distance, onward)
        if distance == 1:
            for da in range(2):
                across(z, da)
        else:
            both(distance - 1, across)
    both(layers - 1, across)
    keep.wait()
    first.wait_send()
    for layer in range(layers):
        for da in range(2):
            spread(layer, da, False, finish)
            hand_over(layer, da, finish)
            for db in range(2):
                arrive(place(layer, da, db, 1 - core))


def gather_blocks(block):
    dp_count, mp_count = lax.axis_size("dp"), lax.axis_size("mp")
    rows, width = block.shape
    if mp_count != 2 or dp_count % 4:
        wide = lax.all_gather(block, "mp", axis=1, tiled=True)
        return lax.all_gather(wide, "dp", axis=0, tiled=True)
    layers = dp_count // 4
    dma = pltpu.SemaphoreType.DMA
    return pl.pallas_call(
        gather_kernel,
        out_shape=jax.ShapeDtypeStruct((dp_count * rows, mp_count * width), block.dtype),
        in_specs=[pl.BlockSpec(memory_space=pl.ANY)],
        out_specs=pl.BlockSpec(memory_space=pl.ANY),
        scratch_shapes=[
            dma,
            dma,
            dma((layers * 2,)),
            dma((layers * 2,)),
            dma((layers * 2,)),
            dma((layers * 4,)),
            dma((dp_count * mp_count,)),
        ],
        compiler_params=pltpu.CompilerParams(collective_id=0, has_side_effects=True),
        name="gather_blocks",
    )(block)


def scatter_kernel(
    parts_ref,
    out_ref,
    mine,
    twin,
    cross,
    rise,
    fall,
    last,
    total,
    load_sem,
    twin_send,
    cross_send,
    z_send,
    last_send,
    twin_recv,
    cross_recv,
    rise_recv,
    fall_recv,
    last_recv,
):
    index = lax.axis_index("dp")
    x = lax.axis_index("mp")
    layers = lax.axis_size("dp") // 4
    z, y, core = index // 4, (index // 2) % 2, index % 2
    rows, width = out_ref.shape
    to_a = (index + core * (2 - 4 * y), x + (1 - core) * (1 - 2 * x))
    to_b = (index + (1 - core) * (2 - 4 * y), x + core * (1 - 2 * x))
    to_twin = (index + 1 - 2 * core, x)
    to_up, to_down = (index + 4, x), (index - 4, x)
    has_up, has_down = z < layers - 1, z > 0

    def view(layer, da, db, which):
        dy = which * da + (1 - which) * db
        dx = (1 - which) * da + which * db
        yy, xx = y + dy * (1 - 2 * y), x + dx * (1 - 2 * x)
        row = (layer * 4 + yy * 2 + which) * rows
        return parts_ref.at[
            pl.ds(pl.multiple_of(row, rows), rows),
            pl.ds(pl.multiple_of(xx * width, width), width),
        ]

    def remote(source, target, send_sem, recv_sem, device):
        return pltpu.make_async_remote_copy(
            src_ref=source,
            dst_ref=target,
            send_sem=send_sem,
            recv_sem=recv_sem,
            device_id=device,
            device_id_type=MESH,
        )

    barrier = pltpu.get_barrier_semaphore()
    for peer in (to_a, to_b, to_twin):
        pl.semaphore_signal(barrier, inc=1, device_id=peer, device_id_type=MESH)

    @pl.when(has_up)
    def _():
        pl.semaphore_signal(barrier, inc=1, device_id=to_up, device_id_type=MESH)

    @pl.when(has_down)
    def _():
        pl.semaphore_signal(barrier, inc=1, device_id=to_down, device_id_type=MESH)

    def outward(run):
        for distance in range(layers - 1, 0, -1):
            for da in range(2):
                @pl.when(z + distance < layers)
                def _():
                    run(z + distance, da, True)

                @pl.when(z >= distance)
                def _():
                    run(z - distance, da, False)

    def home(run):
        for da in (1, 0):
            run(z, da, None)

    def load(layer, da, db):
        slot = (layer * 2 + da) * 2 + db
        return pltpu.make_async_copy(view(layer, da, db, core), mine.at[slot], load_sem.at[slot])

    def to_other_core(layer, da, db):
        slot = (layer * 2 + da) * 2 + db
        return remote(
            view(layer, da, db, 1 - core),
            twin.at[slot],
            twin_send.at[slot],
            twin_recv.at[slot],
            to_twin,
        )

    def to_cross(layer, da):
        pair = layer * 2 + da
        return remote(
            mine.at[pair * 2 + 1], cross.at[pair], cross_send.at[pair], cross_recv.at[pair], to_b
        )

    def upward(layer, da):
        pair = layer * 2 + da
        return remote(mine.at[pair * 2], rise.at[pair], z_send.at[pair], rise_recv.at[pair], to_up)

    def downward(layer, da):
        pair = layer * 2 + da
        return remote(
            mine.at[pair * 2], fall.at[pair], z_send.at[pair], fall_recv.at[pair], to_down
        )

    def to_last():
        return remote(mine.at[(z * 2 + 1) * 2], last, last_send, last_recv, to_a)

    def add(target, *sources):
        step = 16

        def body(turn, carry):
            at = pl.ds(pl.multiple_of(turn * step, step), step)
            value = sources[0][at, :].astype(jnp.float32)
            for source in sources[1:]:
                value = value + source[at, :].astype(jnp.float32)
            target[at, :] = value.astype(target.dtype)
            return carry

        lax.fori_loop(0, rows // step, body, 0)

    for db in (1, 0):
        outward(lambda layer, da, up: load(layer, da, db).start())
        home(lambda layer, da, up: load(layer, da, db).start())
    pl.semaphore_wait(barrier, 3 + has_up.astype(jnp.int32) + has_down.astype(jnp.int32))
    for db in (1, 0):
        outward(lambda layer, da, up: to_other_core(layer, da, db).start())
        home(lambda layer, da, up: to_other_core(layer, da, db).start())

    def pair_up(layer, da, up):
        slot = (layer * 2 + da) * 2 + 1
        load(layer, da, 1).wait()
        to_other_core(layer, da, 1).wait_recv()
        add(mine.at[slot], mine.at[slot], twin.at[slot])
        to_cross(layer, da).start()

    outward(pair_up)
    home(pair_up)

    def collect(layer, da, target):
        pair = layer * 2 + da
        load(layer, da, 0).wait()
        to_other_core(layer, da, 0).wait_recv()
        to_cross(layer, da).wait_recv()
        add(target, mine.at[pair * 2], twin.at[pair * 2], cross.at[pair])

    def pass_on(layer, da, up):
        pair = layer * 2 + da
        collect(layer, da, total)
        if up:
            @pl.when(has_down)
            def _():
                upward(layer, da).wait_recv()
                add(total, total, rise.at[pair])
        else:
            @pl.when(has_up)
            def _():
                downward(layer, da).wait_recv()
                add(total, total, fall.at[pair])
        add(mine.at[pair * 2], total)
        (upward if up else downward)(layer, da).start()

    outward(pass_on)

    def settle(layer, da, up):
        pair = layer * 2 + da
        target = total if da else out_ref
        collect(layer, da, target)

        @pl.when(has_down)
        def _():
            upward(layer, da).wait_recv()
            add(target, target, rise.at[pair])

        @pl.when(has_up)
        def _():
            downward(layer, da).wait_recv()
            add(target, target, fall.at[pair])

        if da:
            add(mine.at[pair * 2], total)
            to_last().start()

    home(settle)
    to_last().wait_recv()
    add(out_ref, out_ref, last)

    def finish(layer, da, up):
        to_other_core(layer, da, 0).wait_send()
        to_other_core(layer, da, 1).wait_send()
        to_cross(layer, da).wait_send()
        if up is not None:
            (upward if up else downward)(layer, da).wait_send()

    outward(finish)
    home(finish)
    to_last().wait_send()


def scatter_sum(parts):
    dp_count, mp_count = lax.axis_size("dp"), lax.axis_size("mp")
    rows, width = parts.shape[0] // dp_count, parts.shape[1] // mp_count
    if mp_count != 2 or dp_count % 4:
        halves = lax.psum_scatter(parts, "mp", scatter_dimension=1, tiled=True)
        return lax.psum_scatter(halves, "dp", scatter_dimension=0, tiled=True)
    pairs = dp_count // 2
    dma = pltpu.SemaphoreType.DMA
    block = (rows, width)
    return pl.pallas_call(
        scatter_kernel,
        out_shape=jax.ShapeDtypeStruct(block, jnp.float32),
        in_specs=[pl.BlockSpec(memory_space=pl.ANY)],
        out_specs=pl.BlockSpec(memory_space=pltpu.VMEM),
        scratch_shapes=[
            pltpu.VMEM((2 * pairs,) + block, jnp.bfloat16),
            pltpu.VMEM((2 * pairs,) + block, jnp.bfloat16),
            pltpu.VMEM((pairs,) + block, jnp.bfloat16),
            pltpu.VMEM((pairs,) + block, jnp.bfloat16),
            pltpu.VMEM((pairs,) + block, jnp.bfloat16),
            pltpu.VMEM(block, jnp.bfloat16),
            pltpu.VMEM(block, jnp.float32),
            dma((2 * pairs,)),
            dma((2 * pairs,)),
            dma((pairs,)),
            dma((pairs,)),
            dma,
            dma((2 * pairs,)),
            dma((pairs,)),
            dma((pairs,)),
            dma((pairs,)),
            dma,
        ],
        compiler_params=pltpu.CompilerParams(
            collective_id=1, has_side_effects=True, vmem_limit_bytes=40 * 1024 * 1024
        ),
        name="scatter_sum",
    )(parts.astype(jnp.bfloat16))


def attention(queries, keys, values, query_seg, query_row, key_seg, key_row, keep_mask):
    scale = HEAD_DIM ** (-0.5)
    scores = (
        lax.dot_general(
            queries, keys, (((1,), (1,)), ((), ())), preferred_element_type=jnp.float32
        )
        * scale
    )
    visible = (query_seg[:, None] == key_seg[None, :]) & (
        (keep_mask[None, :] == 1) | (query_row[:, None] == key_row[None, :])
    )
    masked = jnp.where(visible, scores, NEG)
    top = jnp.max(masked, axis=1, keepdims=True)
    weights = jnp.where(visible, jnp.exp(masked - top), 0.0)
    totals = jnp.sum(weights, axis=1, keepdims=True)
    mixed = jnp.dot(weights.astype(jnp.bfloat16), values, preferred_element_type=jnp.float32)
    return (mixed / totals).astype(jnp.bfloat16)


def local(
    tokens,
    lengths,
    keep_mask,
    routes,
    attention_gain,
    mixture_gain,
    query_gain,
    key_gain,
    query_weight,
    key_weight,
    value_weight,
    output_weight,
    router_weight,
    expert_gate,
    expert_up,
    expert_down,
):
    tok_rows = tokens.shape[0]
    dp_count = lax.axis_size("dp")
    dp_index = lax.axis_index("dp")
    mp_index = lax.axis_index("mp")
    local_width = query_weight.shape[1]
    local_heads = local_width // HEAD_DIM
    share = dp_count // local_heads
    part = dp_index % share
    total_rows = tok_rows * dp_count

    weight_rows = query_weight.shape[0]
    packed = jnp.stack([query_weight, key_weight, value_weight]).reshape(
        3, weight_rows, local_heads, HEAD_DIM
    )
    packed = packed.transpose(2, 1, 0, 3).reshape(local_heads, weight_rows, 3 * HEAD_DIM)
    packed = jnp.repeat(packed, share, axis=0)
    head_weight = lax.all_to_all(packed, "dp", split_axis=0, concat_axis=0, tiled=True)
    head_weight = head_weight.reshape(dp_count * weight_rows, 3 * HEAD_DIM)

    all_tokens, head_weight, late_weight = lax.optimization_barrier(
        (gather_blocks(tokens), head_weight, output_weight)
    )
    all_output_weight = lax.all_gather(late_weight, "dp", axis=1, tiled=True)
    xfloat = all_tokens.astype(jnp.float32)
    all_in = (
        xfloat * lax.rsqrt(jnp.mean(xfloat * xfloat, axis=1, keepdims=True) + EPS) * attention_gain
    ).astype(jnp.bfloat16)
    all_routes = lax.all_gather(routes, "dp", axis=0, tiled=True)
    all_gain = lax.all_gather(mixture_gain, "mp", axis=0, tiled=True)
    all_router = lax.all_gather(router_weight, "mp", axis=0, tiled=True)

    key_row = jnp.arange(total_rows, dtype=jnp.int32)
    key_seg, key_pos = segment_info(lengths, key_row)
    cos_table, sin_table = rope_tables(key_pos)

    def own(array):
        split = array.reshape((local_heads, share, tok_rows) + array.shape[1:])
        taken = lax.dynamic_index_in_dim(split, part, 1, keepdims=False)
        return taken.reshape((local_heads * tok_rows,) + array.shape[1:])

    projected = jnp.dot(all_in, head_weight, preferred_element_type=jnp.float32)
    queries = head_prep(
        own(projected[:, :HEAD_DIM]), query_gain, own(cos_table), own(sin_table)
    )
    keys = head_prep(projected[:, HEAD_DIM : 2 * HEAD_DIM], key_gain, cos_table, sin_table)
    values = projected[:, 2 * HEAD_DIM :].astype(jnp.bfloat16)
    attended = attention(
        queries, keys, values, own(key_seg), own(key_row), key_seg, key_row, keep_mask
    )
    groups = [[head * share + p for head in range(local_heads)] for p in range(share)]
    attended = lax.all_to_all(
        attended.reshape(local_heads, tok_rows, HEAD_DIM),
        "dp",
        split_axis=0,
        concat_axis=0,
        tiled=True,
        axis_index_groups=groups,
    )
    attended = attended.transpose(1, 0, 2).reshape(tok_rows, local_width)
    partial_out = jnp.dot(attended, all_output_weight, preferred_element_type=jnp.float32)
    summed_out = lax.psum_scatter(partial_out, "mp", scatter_dimension=1, tiled=True)
    residual = (tokens.astype(jnp.float32) + summed_out).astype(jnp.bfloat16)
    all_residual = gather_blocks(residual)
    hfloat = all_residual.astype(jnp.float32)
    inverse = lax.rsqrt(jnp.mean(hfloat * hfloat, axis=1, keepdims=True) + EPS)
    mixed_in = (hfloat * all_gain * inverse).astype(jnp.bfloat16)

    own_rows = lax.dynamic_slice_in_dim(all_residual, dp_index * tok_rows, tok_rows, 0)
    own_float = own_rows.astype(jnp.float32)
    own_inverse = lax.rsqrt(jnp.mean(own_float * own_float, axis=1, keepdims=True) + EPS)
    logits = (
        jnp.dot(own_float * all_gain, all_router, precision=lax.Precision.HIGHEST) * own_inverse
    )

    ids = jnp.arange(tok_rows, dtype=jnp.int32)
    earlier = (ids[:, None] < ids[None, :]).astype(jnp.bfloat16)
    slots = jnp.arange(CAP, dtype=jnp.int32)

    def chosen_slots(named):
        before = jnp.dot(
            named.astype(jnp.bfloat16).reshape(-1, tok_rows),
            earlier,
            preferred_element_type=jnp.float32,
        ).reshape(named.shape)
        place = jnp.where(named, before.astype(jnp.int32), -1)
        return place[:, :, None, :] == slots[None, None, :, None]

    exp_local = EXPERTS // dp_count
    gate_local = expert_gate[0]
    up_local = expert_up[0]
    down_local = expert_down[0]
    unit_count = gate_local.shape[1]
    held = max(1, unit_count // FF)
    units = unit_count // held
    first_expert = (mp_index * unit_count) // FF

    own_experts = dp_index * exp_local + first_expert + jnp.arange(held, dtype=jnp.int32)
    block_routes = all_routes.reshape(dp_count, tok_rows, TOPK)
    here = jnp.any(block_routes[:, None] == own_experts[None, :, None, None], axis=3)
    chosen = chosen_slots(here)
    select = chosen.astype(jnp.bfloat16).reshape(dp_count, held * CAP, tok_rows)
    rows_in = lax.dot_general(
        select,
        mixed_in.reshape(dp_count, tok_rows, D),
        (((2,), (1,)), ((0,), (0,))),
        preferred_element_type=jnp.float32,
    ).astype(jnp.bfloat16)
    rows_in = rows_in.reshape(dp_count, held, CAP, D)
    experts = jnp.arange(EXPERTS, dtype=jnp.int32)
    named = jnp.any(routes[:, :, None] == experts[None, None, :], axis=1)
    sigmoid_vals = jax.nn.sigmoid(logits) * named.astype(jnp.float32)
    route_weight = sigmoid_vals / jnp.sum(sigmoid_vals, axis=1, keepdims=True)
    all_weights = lax.all_gather(route_weight, "dp", axis=0, tiled=True)
    outs = []
    for index in range(held):
        rows = rows_in[:, index].reshape(dp_count * CAP, D)
        low, high = index * units, (index + 1) * units
        gate_val = jnp.dot(rows, gate_local[:, low:high], preferred_element_type=jnp.float32)
        up_val = jnp.dot(rows, up_local[:, low:high], preferred_element_type=jnp.float32)
        hidden = (jax.nn.silu(gate_val) * up_val).astype(jnp.bfloat16)
        out = jnp.dot(hidden, down_local[low:high], preferred_element_type=jnp.float32)
        outs.append(out.astype(jnp.bfloat16).reshape(dp_count, CAP, D))
    first_own = dp_index * exp_local + first_expert
    own_weights = lax.dynamic_slice_in_dim(all_weights, first_own, held, 1)
    own_weights = own_weights.reshape(dp_count, tok_rows, held).transpose(0, 2, 1)
    spread = jnp.where(chosen, own_weights[:, :, None, :], 0.0)
    spread_high = spread.astype(jnp.bfloat16)
    spread_low = (spread - spread_high.astype(jnp.float32)).astype(jnp.bfloat16)
    contract = (((1,), (1,)), ((0,), (0,)))
    both = jnp.concatenate([spread_high, spread_low], 2).reshape(
        dp_count, held * 2 * CAP, tok_rows
    )
    out_rows = jnp.concatenate(sum([[out, out] for out in outs], []), axis=1)
    parts = lax.dot_general(both, out_rows, contract, preferred_element_type=jnp.float32)
    mixture = scatter_sum(parts.reshape(total_rows, D))
    return (residual.astype(jnp.float32) + mixture).astype(jnp.bfloat16)


def solution(mesh):
    return jax.shard_map(
        local,
        mesh=mesh,
        in_specs=(
            P("dp", "mp"),
            P(),
            P(),
            P("dp", None),
            P(),
            P("mp"),
            P(),
            P(),
            P("dp", "mp"),
            P("dp", "mp"),
            P("dp", "mp"),
            P("mp", "dp"),
            P("mp", None),
            P("dp", None, "mp"),
            P("dp", None, "mp"),
            P("dp", "mp", None),
        ),
        out_specs=P("dp", "mp"),
        check_vma=False,
    )
```

```python
import jax
import jax.numpy as jnp
from jax import lax
from jax.experimental import pallas as pl
from jax.experimental.pallas import tpu as pltpu
from jax.sharding import PartitionSpec as P

D = 2048
HEAD_DIM = 128
FF = 1024
EXPERTS = 64
TOPK = 8
CAP = 32


EPS = 1e-06
ROPE_BASE = 10000.0
NEG = -1e30


def rope_tables(position):
    halves = HEAD_DIM // 2
    exponent = jnp.arange(halves, dtype=jnp.float32) * (2.0 / HEAD_DIM)
    frequency = jnp.power(jnp.float32(ROPE_BASE), -exponent)
    angle = position.astype(jnp.float32)[:, None] * frequency[None, :]
    cos_table = jnp.cos(angle)
    sin_table = jnp.sin(angle)
    return (jnp.concatenate([cos_table, cos_table], 1), jnp.concatenate([sin_table, sin_table], 1))


def head_prep(projected, head_gain, cos_table, sin_table):
    row_count = projected.shape[0]
    per_head = projected.reshape(row_count, -1, HEAD_DIM)
    normed = (
        per_head * lax.rsqrt(jnp.mean(per_head * per_head, axis=2, keepdims=True) + EPS) * head_gain
    )
    halves = HEAD_DIM // 2
    rotated = jnp.concatenate([-normed[:, :, halves:], normed[:, :, :halves]], 2)
    turned = normed * cos_table[:, None, :] + rotated * sin_table[:, None, :]
    return turned.reshape(row_count, -1).astype(jnp.bfloat16)


def segment_info(lengths, global_row):
    request_end = jnp.cumsum(lengths)
    request_start = request_end - lengths
    segment = jnp.sum((request_end[None, :] <= global_row[:, None]).astype(jnp.int32), axis=1)
    chosen = segment[:, None] == jnp.arange(lengths.shape[0], dtype=jnp.int32)[None, :]
    begin = jnp.sum(jnp.where(chosen, request_start[None, :], 0), axis=1)
    return (segment, global_row - begin)


MESH = pl.DeviceIdType.MESH


def gather_kernel(block_ref, out_ref, local_sem, a_sem, up_sem, down_sem, b_sem, twin_sem, recv_sem):
    index = lax.axis_index("dp")
    x = lax.axis_index("mp")
    layers = lax.axis_size("dp") // 4
    z, y, core = index // 4, (index // 2) % 2, index % 2
    rows, width = block_ref.shape
    to_a = (index + core * (2 - 4 * y), x + (1 - core) * (1 - 2 * x))
    to_b = (index + (1 - core) * (2 - 4 * y), x + core * (1 - 2 * x))
    to_twin = (index + 1 - 2 * core, x)
    to_up, to_down = (index + 4, x), (index - 4, x)

    def place(layer, da, db, which):
        dy = which * da + (1 - which) * db
        dx = (1 - which) * da + which * db
        yy, xx = y + dy * (1 - 2 * y), x + dx * (1 - 2 * x)
        return layer * 4 + yy * 2 + which, xx

    def view(spot):
        return out_ref.at[
            pl.ds(pl.multiple_of(spot[0] * rows, rows), rows),
            pl.ds(pl.multiple_of(spot[1] * width, width), width),
        ]

    def send(spot, sem, device, own=False):
        return pltpu.make_async_remote_copy(
            src_ref=block_ref if own else view(spot),
            dst_ref=view(spot),
            send_sem=sem,
            recv_sem=recv_sem.at[spot[0] * 2 + spot[1]],
            device_id=device,
            device_id_type=MESH,
        )

    def arrive(spot):
        send(spot, local_sem, to_twin).wait_recv()

    barrier = pltpu.get_barrier_semaphore()
    for peer in (to_a, to_b, to_twin):
        pl.semaphore_signal(barrier, inc=1, device_id=peer, device_id_type=MESH)
    has_up, has_down = z < layers - 1, z > 0

    @pl.when(has_up)
    def _():
        pl.semaphore_signal(barrier, inc=1, device_id=to_up, device_id_type=MESH)

    @pl.when(has_down)
    def _():
        pl.semaphore_signal(barrier, inc=1, device_id=to_down, device_id_type=MESH)

    pl.semaphore_wait(
        barrier, 3 + has_up.astype(jnp.int32) + has_down.astype(jnp.int32)
    )

    home = place(z, 0, 0, core)
    keep = pltpu.make_async_copy(block_ref, view(home), local_sem)
    first = send(home, a_sem, to_a, True)

    def spread(layer, da, own, act):
        spot = place(layer, da, 0, core)
        slot = layer * 2 + da

        @pl.when((layer <= z) & has_up)
        def _():
            act(send(spot, up_sem.at[slot], to_up, own))

        @pl.when((layer >= z) & has_down)
        def _():
            act(send(spot, down_sem.at[slot], to_down, own))

        act(send(spot, b_sem.at[slot], to_b, own))
        act(send(spot, twin_sem.at[slot * 2], to_twin, own))

    def hand_over(layer, da, act):
        spot = place(layer, da, 1, core)
        act(send(spot, twin_sem.at[(layer * 2 + da) * 2 + 1], to_twin))

    start = lambda copy: copy.start()
    finish = lambda copy: copy.wait_send()
    first.start()
    spread(z, 0, True, start)
    keep.start()
    arrive(place(z, 1, 0, core))
    spread(z, 1, False, start)

    def both(distance, run):
        for da in range(2):
            @pl.when(z >= distance)
            def _():
                run(z - distance, da)

            @pl.when(z + distance < layers)
            def _():
                run(z + distance, da)

    def onward(layer, da):
        arrive(place(layer, da, 0, core))
        spread(layer, da, False, start)

    def across(layer, da):
        arrive(place(layer, da, 1, core))
        hand_over(layer, da, start)

    for distance in range(1, layers):
        both(distance, onward)
        if distance == 1:
            for da in range(2):
                across(z, da)
        else:
            both(distance - 1, across)
    both(layers - 1, across)
    keep.wait()
    first.wait_send()
    for layer in range(layers):
        for da in range(2):
            spread(layer, da, False, finish)
            hand_over(layer, da, finish)
            for db in range(2):
                arrive(place(layer, da, db, 1 - core))


def gather_blocks(block):
    dp_count, mp_count = lax.axis_size("dp"), lax.axis_size("mp")
    rows, width = block.shape
    if mp_count != 2 or dp_count % 4:
        wide = lax.all_gather(block, "mp", axis=1, tiled=True)
        return lax.all_gather(wide, "dp", axis=0, tiled=True)
    layers = dp_count // 4
    dma = pltpu.SemaphoreType.DMA
    return pl.pallas_call(
        gather_kernel,
        out_shape=jax.ShapeDtypeStruct((dp_count * rows, mp_count * width), block.dtype),
        in_specs=[pl.BlockSpec(memory_space=pl.ANY)],
        out_specs=pl.BlockSpec(memory_space=pl.ANY),
        scratch_shapes=[
            dma,
            dma,
            dma((layers * 2,)),
            dma((layers * 2,)),
            dma((layers * 2,)),
            dma((layers * 4,)),
            dma((dp_count * mp_count,)),
        ],
        compiler_params=pltpu.CompilerParams(collective_id=0, has_side_effects=True),
        name="gather_blocks",
    )(block)


def scatter_kernel(
    parts_ref,
    out_ref,
    mine,
    twin,
    cross,
    rise,
    fall,
    last,
    total,
    load_sem,
    twin_send,
    cross_send,
    z_send,
    last_send,
    twin_recv,
    cross_recv,
    rise_recv,
    fall_recv,
    last_recv,
):
    index = lax.axis_index("dp")
    x = lax.axis_index("mp")
    layers = lax.axis_size("dp") // 4
    z, y, core = index // 4, (index // 2) % 2, index % 2
    rows, width = out_ref.shape
    to_a = (index + core * (2 - 4 * y), x + (1 - core) * (1 - 2 * x))
    to_b = (index + (1 - core) * (2 - 4 * y), x + core * (1 - 2 * x))
    to_twin = (index + 1 - 2 * core, x)
    to_up, to_down = (index + 4, x), (index - 4, x)
    has_up, has_down = z < layers - 1, z > 0

    def view(layer, da, db, which):
        dy = which * da + (1 - which) * db
        dx = (1 - which) * da + which * db
        yy, xx = y + dy * (1 - 2 * y), x + dx * (1 - 2 * x)
        row = (layer * 4 + yy * 2 + which) * rows
        return parts_ref.at[
            pl.ds(pl.multiple_of(row, rows), rows),
            pl.ds(pl.multiple_of(xx * width, width), width),
        ]

    def remote(source, target, send_sem, recv_sem, device):
        return pltpu.make_async_remote_copy(
            src_ref=source,
            dst_ref=target,
            send_sem=send_sem,
            recv_sem=recv_sem,
            device_id=device,
            device_id_type=MESH,
        )

    barrier = pltpu.get_barrier_semaphore()
    for peer in (to_a, to_b, to_twin):
        pl.semaphore_signal(barrier, inc=1, device_id=peer, device_id_type=MESH)

    @pl.when(has_up)
    def _():
        pl.semaphore_signal(barrier, inc=1, device_id=to_up, device_id_type=MESH)

    @pl.when(has_down)
    def _():
        pl.semaphore_signal(barrier, inc=1, device_id=to_down, device_id_type=MESH)

    def outward(run):
        for distance in range(layers - 1, 0, -1):
            for da in range(2):
                @pl.when(z + distance < layers)
                def _():
                    run(z + distance, da, True)

                @pl.when(z >= distance)
                def _():
                    run(z - distance, da, False)

    def home(run):
        for da in (1, 0):
            run(z, da, None)

    def load(layer, da, db):
        slot = (layer * 2 + da) * 2 + db
        return pltpu.make_async_copy(view(layer, da, db, core), mine.at[slot], load_sem.at[slot])

    def to_other_core(layer, da, db):
        slot = (layer * 2 + da) * 2 + db
        return remote(
            view(layer, da, db, 1 - core),
            twin.at[slot],
            twin_send.at[slot],
            twin_recv.at[slot],
            to_twin,
        )

    def to_cross(layer, da):
        pair = layer * 2 + da
        return remote(
            mine.at[pair * 2 + 1], cross.at[pair], cross_send.at[pair], cross_recv.at[pair], to_b
        )

    def upward(layer, da):
        pair = layer * 2 + da
        return remote(mine.at[pair * 2], rise.at[pair], z_send.at[pair], rise_recv.at[pair], to_up)

    def downward(layer, da):
        pair = layer * 2 + da
        return remote(
            mine.at[pair * 2], fall.at[pair], z_send.at[pair], fall_recv.at[pair], to_down
        )

    def to_last():
        return remote(mine.at[(z * 2 + 1) * 2], last, last_send, last_recv, to_a)

    def add(target, *sources):
        step = 16

        def body(turn, carry):
            at = pl.ds(pl.multiple_of(turn * step, step), step)
            value = sources[0][at, :].astype(jnp.float32)
            for source in sources[1:]:
                value = value + source[at, :].astype(jnp.float32)
            target[at, :] = value.astype(target.dtype)
            return carry

        lax.fori_loop(0, rows // step, body, 0)

    for db in (1, 0):
        outward(lambda layer, da, up: load(layer, da, db).start())
        home(lambda layer, da, up: load(layer, da, db).start())
    pl.semaphore_wait(barrier, 3 + has_up.astype(jnp.int32) + has_down.astype(jnp.int32))
    for db in (1, 0):
        outward(lambda layer, da, up: to_other_core(layer, da, db).start())
        home(lambda layer, da, up: to_other_core(layer, da, db).start())

    def pair_up(layer, da, up):
        slot = (layer * 2 + da) * 2 + 1
        load(layer, da, 1).wait()
        to_other_core(layer, da, 1).wait_recv()
        add(mine.at[slot], mine.at[slot], twin.at[slot])
        to_cross(layer, da).start()

    outward(pair_up)
    home(pair_up)

    def collect(layer, da, target):
        pair = layer * 2 + da
        load(layer, da, 0).wait()
        to_other_core(layer, da, 0).wait_recv()
        to_cross(layer, da).wait_recv()
        add(target, mine.at[pair * 2], twin.at[pair * 2], cross.at[pair])

    def pass_on(layer, da, up):
        pair = layer * 2 + da
        collect(layer, da, total)
        if up:
            @pl.when(has_down)
            def _():
                upward(layer, da).wait_recv()
                add(total, total, rise.at[pair])
        else:
            @pl.when(has_up)
            def _():
                downward(layer, da).wait_recv()
                add(total, total, fall.at[pair])
        add(mine.at[pair * 2], total)
        (upward if up else downward)(layer, da).start()

    outward(pass_on)

    def settle(layer, da, up):
        pair = layer * 2 + da
        target = total if da else out_ref
        collect(layer, da, target)

        @pl.when(has_down)
        def _():
            upward(layer, da).wait_recv()
            add(target, target, rise.at[pair])

        @pl.when(has_up)
        def _():
            downward(layer, da).wait_recv()
            add(target, target, fall.at[pair])

        if da:
            add(mine.at[pair * 2], total)
            to_last().start()

    home(settle)
    to_last().wait_recv()
    add(out_ref, out_ref, last)

    def finish(layer, da, up):
        to_other_core(layer, da, 0).wait_send()
        to_other_core(layer, da, 1).wait_send()
        to_cross(layer, da).wait_send()
        if up is not None:
            (upward if up else downward)(layer, da).wait_send()

    outward(finish)
    home(finish)
    to_last().wait_send()


def scatter_sum(parts):
    dp_count, mp_count = lax.axis_size("dp"), lax.axis_size("mp")
    rows, width = parts.shape[0] // dp_count, parts.shape[1] // mp_count
    if mp_count != 2 or dp_count % 4:
        halves = lax.psum_scatter(parts, "mp", scatter_dimension=1, tiled=True)
        return lax.psum_scatter(halves, "dp", scatter_dimension=0, tiled=True)
    pairs = dp_count // 2
    dma = pltpu.SemaphoreType.DMA
    block = (rows, width)
    return pl.pallas_call(
        scatter_kernel,
        out_shape=jax.ShapeDtypeStruct(block, jnp.float32),
        in_specs=[pl.BlockSpec(memory_space=pl.ANY)],
        out_specs=pl.BlockSpec(memory_space=pltpu.VMEM),
        scratch_shapes=[
            pltpu.VMEM((2 * pairs,) + block, jnp.bfloat16),
            pltpu.VMEM((2 * pairs,) + block, jnp.bfloat16),
            pltpu.VMEM((pairs,) + block, jnp.bfloat16),
            pltpu.VMEM((pairs,) + block, jnp.bfloat16),
            pltpu.VMEM((pairs,) + block, jnp.bfloat16),
            pltpu.VMEM(block, jnp.bfloat16),
            pltpu.VMEM(block, jnp.float32),
            dma((2 * pairs,)),
            dma((2 * pairs,)),
            dma((pairs,)),
            dma((pairs,)),
            dma,
            dma((2 * pairs,)),
            dma((pairs,)),
            dma((pairs,)),
            dma((pairs,)),
            dma,
        ],
        compiler_params=pltpu.CompilerParams(
            collective_id=1, has_side_effects=True, vmem_limit_bytes=40 * 1024 * 1024
        ),
        name="scatter_sum",
    )(parts.astype(jnp.bfloat16))


def attention(queries, keys, values, query_seg, query_row, key_seg, key_row, keep_mask):
    scale = HEAD_DIM ** (-0.5)
    scores = (
        lax.dot_general(
            queries, keys, (((1,), (1,)), ((), ())), preferred_element_type=jnp.float32
        )
        * scale
    )
    visible = (query_seg[:, None] == key_seg[None, :]) & (
        (keep_mask[None, :] == 1) | (query_row[:, None] == key_row[None, :])
    )
    masked = jnp.where(visible, scores, NEG)
    top = jnp.max(masked, axis=1, keepdims=True)
    weights = jnp.where(visible, jnp.exp(masked - top), 0.0)
    totals = jnp.sum(weights, axis=1, keepdims=True)
    mixed = jnp.dot(weights.astype(jnp.bfloat16), values, preferred_element_type=jnp.float32)
    return (mixed / totals).astype(jnp.bfloat16)


def local(
    tokens,
    lengths,
    keep_mask,
    routes,
    attention_gain,
    mixture_gain,
    query_gain,
    key_gain,
    query_weight,
    key_weight,
    value_weight,
    output_weight,
    router_weight,
    expert_gate,
    expert_up,
    expert_down,
):
    tok_rows = tokens.shape[0]
    dp_count = lax.axis_size("dp")
    dp_index = lax.axis_index("dp")
    mp_index = lax.axis_index("mp")
    local_width = query_weight.shape[1]
    local_heads = local_width // HEAD_DIM
    share = dp_count // local_heads
    part = dp_index % share
    total_rows = tok_rows * dp_count

    weight_rows = query_weight.shape[0]
    packed = jnp.stack([query_weight, key_weight, value_weight]).reshape(
        3, weight_rows, local_heads, HEAD_DIM
    )
    packed = packed.transpose(2, 1, 0, 3).reshape(local_heads, weight_rows, 3 * HEAD_DIM)
    packed = jnp.repeat(packed, share, axis=0)
    head_weight = lax.all_to_all(packed, "dp", split_axis=0, concat_axis=0, tiled=True)
    head_weight = head_weight.reshape(dp_count * weight_rows, 3 * HEAD_DIM)

    all_tokens, head_weight, late_weight = lax.optimization_barrier(
        (gather_blocks(tokens), head_weight, output_weight)
    )
    all_output_weight = lax.all_gather(late_weight, "dp", axis=1, tiled=True)
    xfloat = all_tokens.astype(jnp.float32)
    all_in = (
        xfloat * lax.rsqrt(jnp.mean(xfloat * xfloat, axis=1, keepdims=True) + EPS) * attention_gain
    ).astype(jnp.bfloat16)
    all_routes = lax.all_gather(routes, "dp", axis=0, tiled=True)
    router_and_gain = jnp.concatenate([router_weight, mixture_gain[:, None]], axis=1)
    router_and_gain = lax.all_gather(router_and_gain, "mp", axis=0, tiled=True)
    all_router, all_gain = router_and_gain[:, :EXPERTS], router_and_gain[:, EXPERTS]

    key_row = jnp.arange(total_rows, dtype=jnp.int32)
    key_seg, key_pos = segment_info(lengths, key_row)
    cos_table, sin_table = rope_tables(key_pos)

    def own(array):
        split = array.reshape((local_heads, share, tok_rows) + array.shape[1:])
        taken = lax.dynamic_index_in_dim(split, part, 1, keepdims=False)
        return taken.reshape((local_heads * tok_rows,) + array.shape[1:])

    projected = jnp.dot(all_in, head_weight, preferred_element_type=jnp.float32)
    queries = head_prep(
        own(projected[:, :HEAD_DIM]), query_gain, own(cos_table), own(sin_table)
    )
    keys = head_prep(projected[:, HEAD_DIM : 2 * HEAD_DIM], key_gain, cos_table, sin_table)
    values = projected[:, 2 * HEAD_DIM :].astype(jnp.bfloat16)
    attended = attention(
        queries, keys, values, own(key_seg), own(key_row), key_seg, key_row, keep_mask
    )
    groups = [[head * share + p for head in range(local_heads)] for p in range(share)]
    attended = lax.all_to_all(
        attended.reshape(local_heads, tok_rows, HEAD_DIM),
        "dp",
        split_axis=0,
        concat_axis=0,
        tiled=True,
        axis_index_groups=groups,
    )
    attended = attended.transpose(1, 0, 2).reshape(tok_rows, local_width)
    partial_out = jnp.dot(attended, all_output_weight, preferred_element_type=jnp.float32)
    summed_out = lax.psum_scatter(partial_out, "mp", scatter_dimension=1, tiled=True)
    residual = (tokens.astype(jnp.float32) + summed_out).astype(jnp.bfloat16)
    all_residual = gather_blocks(residual)
    hfloat = all_residual.astype(jnp.float32)
    inverse = lax.rsqrt(jnp.mean(hfloat * hfloat, axis=1, keepdims=True) + EPS)
    scaled = hfloat * all_gain
    mixed_in = (scaled * inverse).astype(jnp.bfloat16)
    logits = jnp.dot(scaled, all_router, precision=lax.Precision.HIGHEST) * inverse

    ids = jnp.arange(tok_rows, dtype=jnp.int32)
    earlier = (ids[:, None] < ids[None, :]).astype(jnp.bfloat16)
    slots = jnp.arange(CAP, dtype=jnp.int32)

    def chosen_slots(named):
        before = jnp.dot(
            named.astype(jnp.bfloat16).reshape(-1, tok_rows),
            earlier,
            preferred_element_type=jnp.float32,
        ).reshape(named.shape)
        place = jnp.where(named, before.astype(jnp.int32), -1)
        return place[:, :, None, :] == slots[None, None, :, None]

    exp_local = EXPERTS // dp_count
    gate_local = expert_gate[0]
    up_local = expert_up[0]
    down_local = expert_down[0]
    unit_count = gate_local.shape[1]
    held = max(1, unit_count // FF)
    units = unit_count // held
    first_expert = (mp_index * unit_count) // FF

    own_experts = dp_index * exp_local + first_expert + jnp.arange(held, dtype=jnp.int32)
    block_routes = all_routes.reshape(dp_count, tok_rows, TOPK)
    here = jnp.any(block_routes[:, None] == own_experts[None, :, None, None], axis=3)
    chosen = chosen_slots(here)
    select = chosen.astype(jnp.bfloat16).reshape(dp_count, held * CAP, tok_rows)
    rows_in = lax.dot_general(
        select,
        mixed_in.reshape(dp_count, tok_rows, D),
        (((2,), (1,)), ((0,), (0,))),
        preferred_element_type=jnp.float32,
    ).astype(jnp.bfloat16)
    rows_in = rows_in.reshape(dp_count, held, CAP, D)
    experts = jnp.arange(EXPERTS, dtype=jnp.int32)
    named = jnp.any(all_routes[:, :, None] == experts[None, None, :], axis=1)
    sigmoid_vals = jax.nn.sigmoid(logits) * named.astype(jnp.float32)
    all_weights = sigmoid_vals / jnp.sum(sigmoid_vals, axis=1, keepdims=True)
    outs = []
    for index in range(held):
        rows = rows_in[:, index].reshape(dp_count * CAP, D)
        low, high = index * units, (index + 1) * units
        gate_val = jnp.dot(rows, gate_local[:, low:high], preferred_element_type=jnp.float32)
        up_val = jnp.dot(rows, up_local[:, low:high], preferred_element_type=jnp.float32)
        hidden = (jax.nn.silu(gate_val) * up_val).astype(jnp.bfloat16)
        out = jnp.dot(hidden, down_local[low:high], preferred_element_type=jnp.float32)
        outs.append(out.astype(jnp.bfloat16).reshape(dp_count, CAP, D))
    first_own = dp_index * exp_local + first_expert
    own_weights = lax.dynamic_slice_in_dim(all_weights, first_own, held, 1)
    own_weights = own_weights.reshape(dp_count, tok_rows, held).transpose(0, 2, 1)
    spread = jnp.where(chosen, own_weights[:, :, None, :], 0.0)
    spread_high = spread.astype(jnp.bfloat16)
    spread_low = (spread - spread_high.astype(jnp.float32)).astype(jnp.bfloat16)
    contract = (((1,), (1,)), ((0,), (0,)))
    both = jnp.concatenate([spread_high, spread_low], 2).reshape(
        dp_count, held * 2 * CAP, tok_rows
    )
    out_rows = jnp.concatenate(sum([[out, out] for out in outs], []), axis=1)
    parts = lax.dot_general(both, out_rows, contract, preferred_element_type=jnp.float32)
    mixture = scatter_sum(parts.reshape(total_rows, D))
    return (residual.astype(jnp.float32) + mixture).astype(jnp.bfloat16)


def solution(mesh):
    return jax.shard_map(
        local,
        mesh=mesh,
        in_specs=(
            P("dp", "mp"),
            P(),
            P(),
            P("dp", None),
            P(),
            P("mp"),
            P(),
            P(),
            P("dp", "mp"),
            P("dp", "mp"),
            P("dp", "mp"),
            P("mp", "dp"),
            P("mp", None),
            P("dp", None, "mp"),
            P("dp", None, "mp"),
            P("dp", "mp", None),
        ),
        out_specs=P("dp", "mp"),
        check_vma=False,
    )
```
